32 devices in a mesh: row: 8 (over z, y), col: 4 (over x, core).
Axes of the slice: x: 2, y: 2, z: 4, core: 2. Of those that a mesh axis runs over, the one named last changes fastest.
Arguments:
- feature: bfloat16 [128, 1024, 192], P('row', 'col'), may hold values from -6 to 6
- mask: int32 [128, 1024], P('row', 'col'), may hold values from 0 to 1, as said below
- dw_weight: float32 [7, 7, 192], replicated, may hold values from -1.75 to 1.75
- dw_bias: float32 [192], replicated, may hold values from -3 to 3
- ln_gain: float32 [192], replicated, may hold values from 0.25 to 1.75
- ln_bias: float32 [192], replicated, may hold values from -2.5 to 2.5
- w_in: bfloat16 [192, 768], replicated, may hold values from -0.4375 to 0.4375
- b_in: float32 [768], replicated, may hold values from -3 to 3
- w_out: bfloat16 [768, 192], replicated, may hold values from -0.3125 to 0.3125
- b_out: float32 [192], replicated, may hold values from -2.5 to 2.5
- layer_scale: float32 [192], replicated, may hold values from 0.2 to 1.5
- w_key: bfloat16 [192, 192], replicated, may hold values from -0.4375 to 0.4375
- w_value: bfloat16 [192, 192], replicated, may hold values from -0.4375 to 0.4375
- queries: bfloat16 [512, 192], replicated, may hold values from -160 to 160
- w_proj: bfloat16 [192, 192], replicated, may hold values from -0.4375 to 0.4375
Outputs:
- block_out: bfloat16 [128, 1024, 192], P('row', 'col')
- pooled_out: float32 [512, 192], replicated
The draws below stay inside these ranges and needn't reach their ends.
Inputs may be any that keep to these rules, and one draw needn't show every extreme that they name: `mask`: position (0, 0) is tissue; tissue comes in regions, and some devices' blocks hold none.
All inputs are finite; a program needn't handle non-finite values.
Results may differ from the reference program's by a relative error of at most 0.015.
Values may be sent and summed in bfloat16 or wider, within the bound.
A program may use at most 128 MiB of HBM per device.

```python
import math
import jax
import jax.numpy as jnp
from jax import lax

C = 192
FF = 768
Q = 512
NH = 8
DH = 24
RB = 16
CB = 256
H = 128
W = 1024


def draw_mask(key, part):
    base = jax.random.fold_in(key, 11)
    first, second, third = jax.random.split(base, 3)
    device_level = jax.random.randint(first, (H // RB, W // CB), 0, 5)
    region_draw = jax.random.randint(second, (H // 8, W // 128), 0, 4)
    position_draw = jax.random.randint(third, (H, W), 0, 4)
    level_spread = jnp.repeat(jnp.repeat(device_level, RB // 8, axis=0), CB // 128, axis=1)
    region_on = (region_draw < level_spread).astype(jnp.int32)
    region_full = jnp.repeat(jnp.repeat(region_on, 8, axis=0), 128, axis=1)
    tissue = region_full * (position_draw < 3).astype(jnp.int32)
    return tissue.at[0, 0].set(1).astype(jnp.int32)


def draw_queries(key, part):
    base = jax.random.fold_in(key, 5)
    first = jax.random.fold_in(base, 0)
    values = jnp.clip(jax.random.normal(first, (Q, C), jnp.float32), -4.0, 4.0)
    return values.astype(jnp.bfloat16)


def steps_of(key, shape, cuts, low, high):
    gain, own = 1.0, jax.random.fold_in(key, 6)
    for axis_at, blocks in cuts:
        steps = jnp.exp(jax.random.uniform(jax.random.fold_in(own, axis_at), (blocks,), jnp.float32, low / len(cuts), high / len(cuts)))
        gain = gain * jnp.repeat(steps, shape[axis_at] // blocks).reshape([-1 if axis == axis_at else 1 for axis in range(len(shape))])
    return gain


def centred(key, shape, scale, limit, shards=(), kind=jnp.bfloat16):
    entries = jax.random.normal(key, shape, jnp.float32) * scale
    if len(shards) > 0:
        entries = steps_of(key, shape, shards, -0.22, 0.18) * entries
    return jnp.clip(entries, min=-limit, max=limit).astype(kind)


def setup_inputs(seed: int = 0) -> dict:
    streams_of = jax.random.split(jax.random.key(seed), 16)
    return {
        "feature": centred(streams_of[0], (H, W, C), 1.0, 6.0, ((0, 8), (1, 4))),
        "mask": draw_mask(jax.random.fold_in(streams_of[15], 71), 0),
        "dw_weight": centred(streams_of[2], (7, 7, C), 12 ** -0.5, 1.75, (), jnp.float32),
        "dw_bias": centred(streams_of[3], (C,), 0.5, 3.0, (), jnp.float32),
        "ln_gain": jnp.clip(1.0 + 0.15 * jax.random.normal(streams_of[4], (C,), jnp.float32), 0.25, 1.75),
        "ln_bias": centred(streams_of[5], (C,), 0.4, 2.5, (), jnp.float32),
        "w_in": centred(streams_of[6], (C, FF), C ** -0.5, 0.4375),
        "b_in": centred(streams_of[7], (FF,), 0.5, 3.0, (), jnp.float32),
        "w_out": centred(streams_of[8], (FF, C), (FF // 2) ** -0.5, 0.3125),
        "b_out": centred(streams_of[9], (C,), 0.4, 2.5, (), jnp.float32),
        "layer_scale": jnp.clip(jnp.exp(jax.random.uniform(streams_of[10], (C,), jnp.float32, math.log(0.2), math.log(1.5))), 0.2, 1.5),
        "w_key": centred(streams_of[11], (C, C), C ** -0.5, 0.4375),
        "w_value": centred(streams_of[12], (C, C), C ** -0.5, 0.4375),
        "queries": draw_queries(jax.random.fold_in(streams_of[15], 71), 0),
        "w_proj": centred(streams_of[14], (C, C), C ** -0.5, 0.4375),
    }


def convnext_band(padded_band, center, dw_weight, dw_bias, ln_gain, ln_bias, w_in, b_in, w_out, b_out, layer_scale):
    band_rows = center.shape[0]
    band_cols = center.shape[1]
    conv = jnp.zeros(center.shape, jnp.float32)
    for offset_row in range(7):
        for offset_col in range(7):
            window = padded_band[offset_row:offset_row + band_rows, offset_col:offset_col + band_cols, :]
            conv = conv + window.astype(jnp.float32) * dw_weight[offset_row, offset_col]
    conv = conv + dw_bias
    flat = conv.reshape(-1, conv.shape[-1])
    center_flat = center.reshape(-1, center.shape[-1])
    average = lax.optimization_barrier(jnp.mean(flat, axis=-1, keepdims=True))
    spread = lax.optimization_barrier(jnp.mean((flat - average) ** 2, axis=-1, keepdims=True))
    normed = ((flat - average) * lax.rsqrt(spread + 1e-06) * ln_gain + ln_bias).astype(jnp.bfloat16)
    inner = jnp.dot(normed, w_in, preferred_element_type=jnp.float32) + b_in
    hidden = jax.nn.gelu(inner, approximate=False).astype(jnp.bfloat16)
    branch = jnp.dot(hidden, w_out, preferred_element_type=jnp.float32) + b_out
    result = (center_flat.astype(jnp.float32) + layer_scale * branch).astype(jnp.bfloat16)
    return result.reshape(center.shape)

def pool_group(running, key_group, value_group, mask_group, query_heads, heads, head_size):
    top, total, accum = running
    key_tiles = key_group.reshape(-1, 128, heads, head_size).astype(jnp.float32)
    value_tiles = value_group.reshape(-1, 128, heads, head_size).astype(jnp.float32)
    tissue = mask_group.reshape(-1, 128) > 0
    scores = jnp.einsum('qhd,tphd->thqp', query_heads.astype(jnp.float32), key_tiles) * (1.0 / head_size ** 0.5)
    scores = jnp.where(tissue[:, None, None, :], scores, -jnp.inf)
    tile_top = lax.optimization_barrier(jnp.max(scores, axis=-1))
    safe_top = jnp.where(jnp.isfinite(tile_top), tile_top, 0.0)
    weights = jnp.where(tissue[:, None, None, :], jnp.exp(scores - safe_top[..., None]), 0.0).astype(jnp.bfloat16)
    tile_total = lax.optimization_barrier(jnp.sum(weights.astype(jnp.float32), axis=-1))
    tile_accum = jnp.einsum('thqp,tphd->thqd', weights.astype(jnp.float32), value_tiles)
    new_top = jnp.maximum(top, lax.optimization_barrier(jnp.max(tile_top, axis=0)))
    keep = jnp.exp(top - new_top)
    factor = jnp.exp(tile_top - new_top)
    total = total * keep + lax.optimization_barrier(jnp.sum(factor * tile_total, axis=0))
    accum = accum * keep[..., None] + lax.optimization_barrier(jnp.sum(factor[..., None] * tile_accum, axis=0))
    return (new_top, total, accum)

def reference(feature, mask, dw_weight, dw_bias, ln_gain, ln_bias, w_in, b_in, w_out, b_out, layer_scale, w_key, w_value, queries, w_proj):
    padded = jnp.pad(feature, ((3, 3), (3, 3), (0, 0)))
    band_count = H // RB

    def one_band(index):
        start = (index * RB).astype(jnp.int32)
        padded_band = lax.dynamic_slice_in_dim(padded, start, RB + 6, 0)
        center = lax.dynamic_slice_in_dim(feature, start, RB, 0)
        return convnext_band(padded_band, center, dw_weight, dw_bias, ln_gain, ln_bias, w_in, b_in, w_out, b_out, layer_scale)
    block_out = lax.map(one_band, jnp.arange(band_count, dtype=jnp.int32)).reshape(H, W, C)
    flat = block_out.reshape(-1, C)
    keys = jnp.dot(flat, w_key, preferred_element_type=jnp.float32).astype(jnp.bfloat16)
    values = jnp.dot(flat, w_value, preferred_element_type=jnp.float32).astype(jnp.bfloat16)
    query_heads = queries.reshape(Q, NH, DH)
    group_count = H * W // 512
    inputs = (keys.reshape(group_count, 512, C), values.reshape(group_count, 512, C), mask.reshape(group_count, 512))
    start_state = (jnp.full((NH, Q), -1e+30, jnp.float32), jnp.zeros((NH, Q), jnp.float32), jnp.zeros((NH, Q, DH), jnp.float32))

    def advance(running, items):
        return (pool_group(running, items[0], items[1], items[2], query_heads, NH, DH), None)
    final, unused = lax.scan(advance, start_state, inputs)
    pooled = final[2] / final[1][..., None]
    pooled = jnp.transpose(pooled, (1, 0, 2)).reshape(Q, C).astype(jnp.bfloat16)
    pooled_out = jnp.dot(pooled, w_proj, preferred_element_type=jnp.float32)
    return (block_out, pooled_out)
```

```python
import functools
import math

import jax
import jax.numpy as jnp
from jax import lax
from jax.experimental import pallas as pl
from jax.experimental.pallas import tpu as pltpu
from jax.sharding import PartitionSpec as P

NH = 8
PAD = 16
LOW = -1e29
MASKED = -1e30


def block_kernel(
    rows,
    cols,
    channels,
    hidden,
    query_count,
    x_ref,
    bias_ref,
    dw_ref,
    vec_ref,
    win_ref,
    bin_ref,
    wout_ref,
    wkt_ref,
    wv_ref,
    q_ref,
    out_ref,
    part_ref,
    xf_ref,
    conv_ref,
    kt_ref,
    v_ref,
    sa_ref,
    sb_ref,
):
    positions = rows * cols
    head_size = channels // NH
    depth = kt_ref.shape[0]
    wide = 256
    high = channels - 128

    def widen(i, carry):
        line = x_ref[i].astype(jnp.float32)
        xf_ref[0, i] = line[:, 0:128]
        xf_ref[1, i, :, 0:high] = line[:, 128:channels]
        return carry

    lax.fori_loop(0, rows + 6, widen, 0)

    def conv_tile(tile, carry):
        start = pl.multiple_of(tile * 8, 8)
        for half in range(2):
            acc = [None] * rows
            for b in range(7):
                taps = [dw_ref[half, a, b] for a in range(7)]
                for i in range(rows + 6):
                    window = xf_ref[half, i, pl.ds(start + (PAD - 3 + b), 8), :]
                    for a in range(7):
                        r = i - a
                        if 0 <= r < rows:
                            term = window * taps[a]
                            acc[r] = term if acc[r] is None else acc[r] + term
            for r in range(rows):
                conv_ref[r, pl.ds(start, 8), half * 128 : half * 128 + 128] = acc[r]
        return carry

    lax.fori_loop(0, cols // 8, conv_tile, 0)

    block = 2 * cols
    dw_bias = vec_ref[0:1, :]
    gain = vec_ref[1:2, :]
    shift = vec_ref[2:3, :]
    b_out = vec_ref[3:4, :]
    scale = vec_ref[4:5, :]
    kt_ref[channels:depth, :] = jnp.zeros((depth - channels, positions), jnp.bfloat16)
    kt_ref[channels : channels + 16, :] = bias_ref[...]
    lane16 = lax.broadcasted_iota(jnp.int32, (positions, wide - channels), 1)
    v_ref[:, channels:wide] = jnp.where(lane16 < NH, 1.0, 0.0).astype(jnp.bfloat16)

    def mlp(step, carry):
        row = step * 2
        flat = conv_ref[pl.ds(row, 2)].reshape(block, wide)[:, 0:channels] + dw_bias
        center = x_ref[pl.ds(row + 3, 2), PAD : PAD + cols, :].reshape(block, channels)
        average = jnp.mean(flat, axis=-1, keepdims=True)
        moved = flat - average
        spread = jnp.mean(moved * moved, axis=-1, keepdims=True)
        normed = (moved * lax.rsqrt(spread + 1e-06) * gain + shift).astype(jnp.bfloat16)
        inner = jnp.dot(normed, win_ref[...], preferred_element_type=jnp.float32) + bin_ref[...]
        act = (0.5 * inner * (1.0 + lax.erf(inner * math.sqrt(0.5)))).astype(jnp.bfloat16)
        branch = jnp.dot(act, wout_ref[...], preferred_element_type=jnp.float32) + b_out
        result = (center.astype(jnp.float32) + scale * branch).astype(jnp.bfloat16)
        out_ref[pl.ds(row, 2)] = result.reshape(2, cols, channels)
        first = pl.multiple_of(step * block, block)
        kt_ref[0:channels, pl.ds(first, block)] = lax.dot_general(
            wkt_ref[...], result, (((1,), (1,)), ((), ())), preferred_element_type=jnp.float32
        ).astype(jnp.bfloat16)
        v_ref[pl.ds(first, block), 0:channels] = jnp.dot(
            result, wv_ref[...], preferred_element_type=jnp.float32
        ).astype(jnp.bfloat16)
        return carry

    lax.fori_loop(0, rows // 2, mlp, 0)

    factor = math.log2(math.e) / math.sqrt(head_size)
    qb = sa_ref.shape[0]
    blocks = query_count // qb
    total = NH * blocks
    lane = lax.broadcasted_iota(jnp.int32, (qb, wide), 1)
    owner = jnp.where(
        lane < channels,
        lane // head_size,
        jnp.where(lane < channels + NH, lane - channels, NH),
    )

    def score(index, s_ref):
        first = pl.multiple_of(index * qb, qb)
        s = jnp.dot(
            q_ref[pl.ds(first, qb), :], kt_ref[...], preferred_element_type=jnp.float32
        )
        s_ref[...] = s
        return jnp.maximum(jnp.max(s, axis=-1, keepdims=True), LOW)

    def absorb(index, s_ref, top):
        e = jnp.exp2((s_ref[...] - top) * factor).astype(jnp.bfloat16)
        o = jnp.dot(e, v_ref[...], preferred_element_type=jnp.float32)
        head = index // blocks
        at = pl.multiple_of((index - head * blocks) * qb, qb)
        held = part_ref[pl.ds(at, qb), :]
        held = jnp.where(owner == head, o, held)
        held = jnp.where(lane == channels + NH + head, top * factor, held)
        part_ref[pl.ds(at, qb), :] = held

    part_ref[...] = jnp.zeros_like(part_ref)
    top_a = score(0, sa_ref)

    def attend(pair, top_a):
        index = pair * 2
        top_b = score(index + 1, sb_ref)
        absorb(index, sa_ref, top_a)
        top_a = score(jnp.minimum(index + 2, total - 1), sa_ref)
        absorb(index + 1, sb_ref, top_b)
        return top_a

    lax.fori_loop(0, total // 2, attend, top_a)


def halo(value, axis, dim, width):
    count, length = (lax.axis_size(axis), value.shape[dim])
    up = [(i, i + 1) for i in range(count - 1)]
    down = [(j, i) for i, j in up]
    last = lax.slice_in_dim(value, length - width, length, axis=dim)
    initial = lax.slice_in_dim(value, 0, width, axis=dim)
    before = lax.ppermute(last, axis, up)
    after = lax.ppermute(initial, axis, down)
    return jnp.concatenate([before, value, after], axis=dim)


def body(
    feature,
    mask,
    dw_weight,
    dw_bias,
    ln_gain,
    ln_bias,
    w_in,
    b_in,
    w_out,
    b_out,
    layer_scale,
    w_key,
    w_value,
    queries,
    w_proj,
):
    rows, cols, channels = feature.shape
    positions = rows * cols
    hidden = w_in.shape[1]
    query_count = queries.shape[0]
    head_size = channels // NH
    depth = channels + 16
    padded = halo(halo(feature, "row", 0, 3), "col", 1, PAD)
    bias = jnp.where(mask > 0, 0.0, MASKED).astype(jnp.bfloat16).reshape(1, positions)
    bias = jnp.pad(bias, ((0, 15), (0, 0)))
    dw = jnp.pad(dw_weight, ((0, 0), (0, 0), (0, 256 - channels)))
    dw = jnp.transpose(dw.reshape(7, 7, 2, 128), (2, 0, 1, 3))
    dw = jnp.broadcast_to(dw[:, :, :, None, :], (2, 7, 7, 8, 128))
    vectors = jnp.stack([dw_bias, ln_gain, ln_bias, b_out, layer_scale] + [b_out] * 3)
    channel_head = jnp.arange(channels) // head_size
    own = channel_head[None, :] == jnp.arange(NH)[:, None]
    spread = jnp.where(own[:, None, :], queries[None], 0).astype(jnp.bfloat16)
    tail = jnp.where(jnp.arange(depth - channels) == 0, 1.0, 0.0).astype(jnp.bfloat16)
    tail = jnp.broadcast_to(tail, (NH, query_count, depth - channels))
    q_wide = jnp.concatenate([spread, tail], axis=-1).reshape(NH * query_count, depth)
    qb = 256
    whole = pl.BlockSpec(memory_space=pltpu.VMEM)
    block_out, part = pl.pallas_call(
        functools.partial(block_kernel, rows, cols, channels, hidden, query_count),
        out_shape=(
            jax.ShapeDtypeStruct(feature.shape, jnp.bfloat16),
            jax.ShapeDtypeStruct((query_count, 256), jnp.float32),
        ),
        in_specs=[whole] * 10,
        out_specs=(whole, whole),
        scratch_shapes=[
            pltpu.VMEM((2, rows + 6, cols + 2 * PAD, 128), jnp.float32),
            pltpu.VMEM((rows, cols, 256), jnp.float32),
            pltpu.VMEM((depth, positions), jnp.bfloat16),
            pltpu.VMEM((positions, 256), jnp.bfloat16),
            pltpu.VMEM((qb, positions), jnp.float32),
            pltpu.VMEM((qb, positions), jnp.float32),
        ],
        compiler_params=pltpu.CompilerParams(vmem_limit_bytes=56 << 20),
        name="block",
    )(
        padded,
        bias,
        dw,
        vectors,
        w_in,
        b_in.reshape(1, hidden),
        w_out,
        jnp.transpose(w_key),
        w_value,
        q_wide,
    )
    top = part[:, channels + NH : channels + 2 * NH]
    best = lax.pmax(top, ("row", "col"))
    keep = jnp.exp2(top - best)
    scaled = jnp.concatenate(
        [
            part[:, :channels] * jnp.repeat(keep, head_size, axis=1),
            part[:, channels : channels + NH] * keep,
        ],
        axis=1,
    )
    merged = lax.psum(scaled, ("row", "col"))
    pooled = merged[:, :channels] / jnp.repeat(merged[:, channels:], head_size, axis=1)
    pooled_out = jnp.dot(
        pooled.astype(jnp.bfloat16), w_proj, preferred_element_type=jnp.float32
    )
    return (block_out, pooled_out)


def solution(mesh):
    return jax.shard_map(
        body,
        mesh=mesh,
        in_specs=(P("row", "col", None), P("row", "col")) + (P(),) * 13,
        out_specs=(P("row", "col", None), P()),
        check_vma=False,
    )
```

```python
import functools
import math

import jax
import jax.numpy as jnp
from jax import lax
from jax.experimental import pallas as pl
from jax.experimental.pallas import tpu as pltpu
from jax.sharding import PartitionSpec as P

NH = 8
PAD = 16
LOW = -1e29
MASKED = -1e30


def block_kernel(
    rows,
    cols,
    channels,
    hidden,
    query_count,
    x_ref,
    bias_ref,
    dw_ref,
    vec_ref,
    win_ref,
    bin_ref,
    wout_ref,
    wkt_ref,
    wv_ref,
    q_ref,
    out_ref,
    part_ref,
    xf_ref,
    conv_ref,
    kt_ref,
    v_ref,
    sa_ref,
    sb_ref,
):
    positions = rows * cols
    head_size = channels // NH
    depth = kt_ref.shape[0]
    wide = 256
    high = channels - 128

    def widen(i, carry):
        line = x_ref[i].astype(jnp.float32)
        xf_ref[0, i] = line[:, 0:128]
        xf_ref[1, i, :, 0:high] = line[:, 128:channels]
        return carry

    lax.fori_loop(0, rows + 6, widen, 0)

    def conv_tile(tile, carry):
        start = pl.multiple_of(tile * 8, 8)
        for half in range(2):
            acc = [None] * rows
            for b in range(7):
                taps = [dw_ref[half, a, b] for a in range(7)]
                for i in range(rows + 6):
                    window = xf_ref[half, i, pl.ds(start + (PAD - 3 + b), 8), :]
                    for a in range(7):
                        r = i - a
                        if 0 <= r < rows:
                            term = window * taps[a]
                            acc[r] = term if acc[r] is None else acc[r] + term
            for r in range(rows):
                conv_ref[r, pl.ds(start, 8), half * 128 : half * 128 + 128] = acc[r]
        return carry

    lax.fori_loop(0, cols // 8, conv_tile, 0)

    block = 2 * cols
    dw_bias = vec_ref[0:1, :]
    gain = vec_ref[1:2, :]
    shift = vec_ref[2:3, :]
    b_out = vec_ref[3:4, :]
    scale = vec_ref[4:5, :]
    kt_ref[channels:depth, :] = jnp.zeros((depth - channels, positions), jnp.bfloat16)
    kt_ref[channels : channels + 16, :] = bias_ref[...]
    lane16 = lax.broadcasted_iota(jnp.int32, (positions, wide - channels), 1)
    v_ref[:, channels:wide] = jnp.where(lane16 < NH, 1.0, 0.0).astype(jnp.bfloat16)

    def mlp(step, carry):
        row = step * 2
        flat = conv_ref[pl.ds(row, 2)].reshape(block, wide)[:, 0:channels] + dw_bias
        center = x_ref[pl.ds(row + 3, 2), PAD : PAD + cols, :].reshape(block, channels)
        average = jnp.mean(flat, axis=-1, keepdims=True)
        moved = flat - average
        spread = jnp.mean(moved * moved, axis=-1, keepdims=True)
        normed = (moved * lax.rsqrt(spread + 1e-06) * gain + shift).astype(jnp.bfloat16)
        inner = jnp.dot(normed, win_ref[...], preferred_element_type=jnp.float32) + bin_ref[...]
        act = (0.5 * inner * (1.0 + lax.erf(inner * math.sqrt(0.5)))).astype(jnp.bfloat16)
        branch = jnp.dot(act, wout_ref[...], preferred_element_type=jnp.float32) + b_out
        result = (center.astype(jnp.float32) + scale * branch).astype(jnp.bfloat16)
        out_ref[pl.ds(row, 2)] = result.reshape(2, cols, channels)
        first = pl.multiple_of(step * block, block)
        kt_ref[0:channels, pl.ds(first, block)] = lax.dot_general(
            wkt_ref[...], result, (((1,), (1,)), ((), ())), preferred_element_type=jnp.float32
        ).astype(jnp.bfloat16)
        v_ref[pl.ds(first, block), 0:channels] = jnp.dot(
            result, wv_ref[...], preferred_element_type=jnp.float32
        ).astype(jnp.bfloat16)
        return carry

    lax.fori_loop(0, rows // 2, mlp, 0)

    factor = math.log2(math.e) / math.sqrt(head_size)
    qb = sa_ref.shape[0]
    blocks = query_count // qb
    total = NH * blocks
    lane = lax.broadcasted_iota(jnp.int32, (qb, wide), 1)
    owner = jnp.where(
        lane < channels,
        lane // head_size,
        jnp.where(lane < channels + NH, lane - channels, NH),
    )

    def score(index, s_ref):
        first = pl.multiple_of(index * qb, qb)
        s = jnp.dot(
            q_ref[pl.ds(first, qb), :], kt_ref[...], preferred_element_type=jnp.float32
        )
        s_ref[...] = s
        return jnp.maximum(jnp.max(s, axis=-1, keepdims=True), LOW)

    def absorb(index, s_ref, top):
        e = jnp.exp2((s_ref[...] - top) * factor).astype(jnp.bfloat16)
        o = jnp.dot(e, v_ref[...], preferred_element_type=jnp.float32)
        head = index // blocks
        at = pl.multiple_of((index - head * blocks) * qb, qb)
        held = part_ref[pl.ds(at, qb), :]
        held = jnp.where(owner == head, o, held)
        held = jnp.where(lane == channels + NH + head, top * factor, held)
        part_ref[pl.ds(at, qb), :] = held

    part_ref[...] = jnp.zeros_like(part_ref)
    top_a = score(0, sa_ref)

    def attend(pair, top_a):
        index = pair * 2
        top_b = score(index + 1, sb_ref)
        absorb(index, sa_ref, top_a)
        top_a = score(jnp.minimum(index + 2, total - 1), sa_ref)
        absorb(index + 1, sb_ref, top_b)
        return top_a

    lax.fori_loop(0, total // 2, attend, top_a)


MESH = pl.DeviceIdType.MESH


def join(packed, owner, low, high):
    top = packed[0]
    for other in packed[1:]:
        top = jnp.maximum(top, other)
    total = None
    for piece in packed:
        keep = jnp.exp2(piece - top)
        factor = jnp.ones_like(piece)
        for head in range(NH):
            factor = jnp.where(owner == head, keep[:, high + head : high + head + 1], factor)
        term = piece * factor
        total = term if total is None else total + term
    lane = lax.broadcasted_iota(jnp.int32, total.shape, 1)
    return jnp.where(lane >= high, top, total)


def owners(shape, channels):
    lane = lax.broadcasted_iota(jnp.int32, shape, 1)
    return jnp.where(
        lane < channels,
        lane // (channels // NH),
        jnp.where(lane < channels + NH, lane - channels, NH),
    )


def merge_kernel(
    nr,
    nc,
    channels,
    part_ref,
    out_ref,
    col_buf,
    mid,
    row_buf,
    gathered,
    send_1,
    recv_1,
    send_2,
    recv_2,
    send_3,
    recv_3,
    send_4,
    recv_4,
):
    r, c = lax.axis_index("row"), lax.axis_index("col")
    count_r = part_ref.shape[1] // nr
    barrier = pltpu.get_barrier_semaphore()
    for k in range(1, nc):
        pl.semaphore_signal(
            barrier, inc=1, device_id=(r, lax.rem(c + k, nc)), device_id_type=MESH
        )
    for k in range(1, nr):
        pl.semaphore_signal(
            barrier, inc=1, device_id=(lax.rem(r + k, nr), c), device_id_type=MESH
        )
    pl.semaphore_wait(barrier, nc + nr - 2)

    def spread(src, dst, send, recv, count, along_col):
        copies = []
        for k in range(1, count):
            peer = lax.rem((c if along_col else r) + k, count)
            copy = pltpu.make_async_remote_copy(
                src_ref=src(peer),
                dst_ref=dst(k),
                send_sem=send.at[k - 1],
                recv_sem=recv.at[k - 1],
                device_id=(r, peer) if along_col else (peer, c),
                device_id_type=MESH,
            )
            copy.start()
            copies.append(copy)
        return copies

    low, high = channels, channels + NH
    first = spread(lambda p: part_ref.at[p], lambda k: col_buf.at[k - 1], send_1, recv_1, nc, True)
    for copy in first:
        copy.wait()
    owner = owners(part_ref.shape[1:], channels)
    pieces = [part_ref[c]] + [col_buf[k] for k in range(nc - 1)]
    total = join(pieces, owner, low, high)
    for j in range(nr):
        mid[j] = total[j * count_r : (j + 1) * count_r]
    second = spread(lambda p: mid.at[p], lambda k: row_buf.at[k - 1], send_2, recv_2, nr, False)
    for copy in second:
        copy.wait()
    owner = owners(mid.shape[1:], channels)
    pieces = [mid[r]] + [row_buf[k] for k in range(nr - 1)]
    total = join(pieces, owner, low, high)
    divisor = jnp.ones_like(total)
    for head in range(NH):
        divisor = jnp.where(owner == head, total[:, low + head : low + head + 1], divisor)
    pooled = total / divisor
    gathered[c, r] = pooled[:, 0:channels].astype(jnp.bfloat16)
    third = spread(
        lambda p: gathered.at[c, r], lambda k: gathered.at[c, r], send_3, recv_3, nr, False
    )
    for copy in third:
        copy.wait()
    fourth = spread(lambda p: gathered.at[c], lambda k: gathered.at[c], send_4, recv_4, nc, True)
    for copy in fourth:
        copy.wait()
    out_ref[...] = gathered[...]


def merged(part, channels):
    nr, nc = lax.axis_size("row"), lax.axis_size("col")
    count_c = part.shape[0] // nc
    count_r = count_c // nr
    wide = part.shape[1]
    whole = pl.BlockSpec(memory_space=pltpu.VMEM)
    sems = []
    for n in (nc, nr, nr, nc):
        sems += [pltpu.SemaphoreType.DMA((n - 1,))] * 2
    pooled = pl.pallas_call(
        functools.partial(merge_kernel, nr, nc, channels),
        out_shape=jax.ShapeDtypeStruct((nc, nr, count_r, channels), jnp.bfloat16),
        in_specs=[whole],
        out_specs=whole,
        scratch_shapes=[
            pltpu.VMEM((nc - 1, count_c, wide), jnp.float32),
            pltpu.VMEM((nr, count_r, wide), jnp.float32),
            pltpu.VMEM((nr - 1, count_r, wide), jnp.float32),
            pltpu.VMEM((nc, nr, count_r, channels), jnp.bfloat16),
        ]
        + sems,
        compiler_params=pltpu.CompilerParams(collective_id=0, has_side_effects=True),
        name="merge",
    )(part.reshape(nc, count_c, wide))
    return pooled.reshape(part.shape[0], channels)


def halo(value, axis, dim, width):
    count, length = (lax.axis_size(axis), value.shape[dim])
    up = [(i, i + 1) for i in range(count - 1)]
    down = [(j, i) for i, j in up]
    last = lax.slice_in_dim(value, length - width, length, axis=dim)
    initial = lax.slice_in_dim(value, 0, width, axis=dim)
    before = lax.ppermute(last, axis, up)
    after = lax.ppermute(initial, axis, down)
    return jnp.concatenate([before, value, after], axis=dim)


def body(
    feature,
    mask,
    dw_weight,
    dw_bias,
    ln_gain,
    ln_bias,
    w_in,
    b_in,
    w_out,
    b_out,
    layer_scale,
    w_key,
    w_value,
    queries,
    w_proj,
):
    rows, cols, channels = feature.shape
    positions = rows * cols
    hidden = w_in.shape[1]
    query_count = queries.shape[0]
    head_size = channels // NH
    depth = channels + 16
    padded = halo(halo(feature, "row", 0, 3), "col", 1, PAD)
    bias = jnp.where(mask > 0, 0.0, MASKED).astype(jnp.bfloat16).reshape(1, positions)
    bias = jnp.pad(bias, ((0, 15), (0, 0)))
    dw = jnp.pad(dw_weight, ((0, 0), (0, 0), (0, 256 - channels)))
    dw = jnp.transpose(dw.reshape(7, 7, 2, 128), (2, 0, 1, 3))
    dw = jnp.broadcast_to(dw[:, :, :, None, :], (2, 7, 7, 8, 128))
    vectors = jnp.stack([dw_bias, ln_gain, ln_bias, b_out, layer_scale] + [b_out] * 3)
    channel_head = jnp.arange(channels) // head_size
    own = channel_head[None, :] == jnp.arange(NH)[:, None]
    spread = jnp.where(own[:, None, :], queries[None], 0).astype(jnp.bfloat16)
    tail = jnp.where(jnp.arange(depth - channels) == 0, 1.0, 0.0).astype(jnp.bfloat16)
    tail = jnp.broadcast_to(tail, (NH, query_count, depth - channels))
    q_wide = jnp.concatenate([spread, tail], axis=-1).reshape(NH * query_count, depth)
    qb = 256
    whole = pl.BlockSpec(memory_space=pltpu.VMEM)
    block_out, part = pl.pallas_call(
        functools.partial(block_kernel, rows, cols, channels, hidden, query_count),
        out_shape=(
            jax.ShapeDtypeStruct(feature.shape, jnp.bfloat16),
            jax.ShapeDtypeStruct((query_count, 256), jnp.float32),
        ),
        in_specs=[whole] * 10,
        out_specs=(whole, whole),
        scratch_shapes=[
            pltpu.VMEM((2, rows + 6, cols + 2 * PAD, 128), jnp.float32),
            pltpu.VMEM((rows, cols, 256), jnp.float32),
            pltpu.VMEM((depth, positions), jnp.bfloat16),
            pltpu.VMEM((positions, 256), jnp.bfloat16),
            pltpu.VMEM((qb, positions), jnp.float32),
            pltpu.VMEM((qb, positions), jnp.float32),
        ],
        compiler_params=pltpu.CompilerParams(vmem_limit_bytes=56 << 20),
        name="block",
    )(
        padded,
        bias,
        dw,
        vectors,
        w_in,
        b_in.reshape(1, hidden),
        w_out,
        jnp.transpose(w_key),
        w_value,
        q_wide,
    )
    pooled_out = jnp.dot(
        merged(part, channels), w_proj, preferred_element_type=jnp.float32
    )
    return (block_out, pooled_out)


def solution(mesh):
    return jax.shard_map(
        body,
        mesh=mesh,
        in_specs=(P("row", "col", None), P("row", "col")) + (P(),) * 13,
        out_specs=(P("row", "col", None), P()),
        check_vma=False,
    )
```

```python
import functools
import math

import jax
import jax.numpy as jnp
from jax import lax
from jax.experimental import pallas as pl
from jax.experimental.pallas import tpu as pltpu
from jax.sharding import PartitionSpec as P

NH = 8
PAD = 16
LOW = -1e29
MASKED = -1e30


def block_kernel(
    rows,
    cols,
    channels,
    hidden,
    query_count,
    x_ref,
    above_ref,
    below_ref,
    left_ref,
    right_ref,
    bias_ref,
    dw_raw_ref,
    dw_bias_ref,
    gain_ref,
    shift_ref,
    b_out_ref,
    scale_ref,
    win_ref,
    bin_ref,
    wout_ref,
    wk_ref,
    wv_ref,
    q_raw_ref,
    out_ref,
    part_ref,
    dw_ref,
    q_ref,
    wkt_ref,
    xf_ref,
    conv_ref,
    kt_ref,
    v_ref,
    sa_ref,
    sb_ref,
):
    positions = rows * cols
    head_size = channels // NH
    depth = kt_ref.shape[0]
    wide = 256
    high = channels - 128

    def place(i, start, size, line):
        line = line.astype(jnp.float32)
        xf_ref[0, i, start : start + size] = line[:, 0:128]
        xf_ref[1, i, start : start + size, 0:high] = line[:, 128:channels]

    def widen(i, carry):
        place(i + 3, PAD, cols, x_ref[i])
        return carry

    def sides(i, carry):
        place(i, 0, PAD, left_ref[i])
        place(i, PAD + cols, PAD, right_ref[i])
        return carry

    lax.fori_loop(0, rows, widen, 0)
    lax.fori_loop(0, rows + 6, sides, 0)
    for i in range(3):
        place(i, PAD, cols, above_ref[i])
        place(rows + 3 + i, PAD, cols, below_ref[i])
    for i in range(7):
        for j in range(7):
            dw_ref[0, i, j] = jnp.broadcast_to(dw_raw_ref[i, j : j + 1, 0:128], (8, 128))
            dw_ref[1, i, j, :, 0:high] = jnp.broadcast_to(
                dw_raw_ref[i, j : j + 1, 128:channels], (8, high)
            )
    wkt_ref[...] = jnp.transpose(wk_ref[...].astype(jnp.float32)).astype(jnp.bfloat16)
    q_lane = lax.broadcasted_iota(jnp.int32, (query_count, channels), 1) // head_size
    tail_lane = lax.broadcasted_iota(jnp.int32, (query_count, depth - channels), 1)
    q_tail = jnp.where(tail_lane == 0, 1.0, 0.0).astype(jnp.bfloat16)
    q_all = q_raw_ref[...].astype(jnp.float32)
    for head in range(NH):
        at = head * query_count
        own = jnp.where(q_lane == head, q_all, 0.0).astype(jnp.bfloat16)
        q_ref[at : at + query_count, 0:channels] = own
        q_ref[at : at + query_count, channels:depth] = q_tail

    def conv_tile(tile, carry):
        start = pl.multiple_of(tile * 8, 8)
        for half in range(2):
            acc = [None] * rows
            for b in range(7):
                taps = [dw_ref[half, a, b] for a in range(7)]
                for i in range(rows + 6):
                    window = xf_ref[half, i, pl.ds(start + (PAD - 3 + b), 8), :]
                    for a in range(7):
                        r = i - a
                        if 0 <= r < rows:
                            term = window * taps[a]
                            acc[r] = term if acc[r] is None else acc[r] + term
            for r in range(rows):
                conv_ref[r, pl.ds(start, 8), half * 128 : half * 128 + 128] = acc[r]
        return carry

    lax.fori_loop(0, cols // 8, conv_tile, 0)

    block = 2 * cols
    dw_bias = dw_bias_ref[...][None, :]
    gain = gain_ref[...][None, :]
    shift = shift_ref[...][None, :]
    b_out = b_out_ref[...][None, :]
    scale = scale_ref[...][None, :]
    b_in = bin_ref[...][None, :]
    kt_ref[channels:depth, :] = jnp.zeros((depth - channels, positions), jnp.bfloat16)
    kt_ref[channels : channels + 16, :] = bias_ref[...]
    lane16 = lax.broadcasted_iota(jnp.int32, (positions, wide - channels), 1)
    v_ref[:, channels:wide] = jnp.where(lane16 < NH, 1.0, 0.0).astype(jnp.bfloat16)

    def mlp(step, carry):
        row = step * 2
        flat = conv_ref[pl.ds(row, 2)].reshape(block, wide)[:, 0:channels] + dw_bias
        center = x_ref[pl.ds(row, 2)].reshape(block, channels)
        average = jnp.mean(flat, axis=-1, keepdims=True)
        moved = flat - average
        spread = jnp.mean(moved * moved, axis=-1, keepdims=True)
        normed = (moved * lax.rsqrt(spread + 1e-06) * gain + shift).astype(jnp.bfloat16)
        inner = jnp.dot(normed, win_ref[...], preferred_element_type=jnp.float32) + b_in
        act = (0.5 * inner * (1.0 + lax.erf(inner * math.sqrt(0.5)))).astype(jnp.bfloat16)
        branch = jnp.dot(act, wout_ref[...], preferred_element_type=jnp.float32) + b_out
        summed = center.astype(jnp.float32) + scale * branch
        result = summed.astype(jnp.bfloat16)
        for i in range(2):
            line = jnp.transpose(summed[i * cols : (i + 1) * cols])
            out_ref[row + i] = line.astype(jnp.bfloat16)
        first = pl.multiple_of(step * block, block)
        kt_ref[0:channels, pl.ds(first, block)] = lax.dot_general(
            wkt_ref[...], result, (((1,), (1,)), ((), ())), preferred_element_type=jnp.float32
        ).astype(jnp.bfloat16)
        v_ref[pl.ds(first, block), 0:channels] = jnp.dot(
            result, wv_ref[...], preferred_element_type=jnp.float32
        ).astype(jnp.bfloat16)
        return carry

    lax.fori_loop(0, rows // 2, mlp, 0)

    factor = math.log2(math.e) / math.sqrt(head_size)
    qb = sa_ref.shape[0]
    blocks = query_count // qb
    total = NH * blocks
    lane = lax.broadcasted_iota(jnp.int32, (qb, wide), 1)
    owner = jnp.where(
        lane < channels,
        lane // head_size,
        jnp.where(lane < channels + NH, lane - channels, NH),
    )

    def score(index, s_ref):
        first = pl.multiple_of(index * qb, qb)
        s = jnp.dot(
            q_ref[pl.ds(first, qb), :], kt_ref[...], preferred_element_type=jnp.float32
        )
        s_ref[...] = s
        return jnp.maximum(jnp.max(s, axis=-1, keepdims=True), LOW)

    def absorb(index, s_ref, top):
        e = jnp.exp2((s_ref[...] - top) * factor).astype(jnp.bfloat16)
        o = jnp.dot(e, v_ref[...], preferred_element_type=jnp.float32)
        head = index // blocks
        at = pl.multiple_of((index - head * blocks) * qb, qb)
        held = part_ref[pl.ds(at, qb), :]
        held = jnp.where(owner == head, o, held)
        held = jnp.where(lane == channels + NH + head, top * factor, held)
        part_ref[pl.ds(at, qb), :] = held

    part_ref[...] = jnp.zeros_like(part_ref)
    top_a = score(0, sa_ref)

    def attend(pair, top_a):
        index = pair * 2
        top_b = score(index + 1, sb_ref)
        absorb(index, sa_ref, top_a)
        top_a = score(jnp.minimum(index + 2, total - 1), sa_ref)
        absorb(index + 1, sb_ref, top_b)
        return top_a

    lax.fori_loop(0, total // 2, attend, top_a)


MESH = pl.DeviceIdType.MESH


def join(packed, owner, low, high):
    top = packed[0]
    for other in packed[1:]:
        top = jnp.maximum(top, other)
    total = None
    for piece in packed:
        keep = jnp.exp2(piece - top)
        factor = jnp.ones_like(piece)
        for head in range(NH):
            factor = jnp.where(owner == head, keep[:, high + head : high + head + 1], factor)
        term = piece * factor
        total = term if total is None else total + term
    lane = lax.broadcasted_iota(jnp.int32, total.shape, 1)
    return jnp.where(lane >= high, top, total)


def owners(shape, channels):
    lane = lax.broadcasted_iota(jnp.int32, shape, 1)
    return jnp.where(
        lane < channels,
        lane // (channels // NH),
        jnp.where(lane < channels + NH, lane - channels, NH),
    )


def merge_kernel(
    nr,
    nc,
    channels,
    part_ref,
    out_ref,
    col_buf,
    mid,
    row_buf,
    gathered,
    send_1,
    recv_1,
    send_2,
    recv_2,
    send_3,
    recv_3,
    send_4,
    recv_4,
):
    r, c = lax.axis_index("row"), lax.axis_index("col")
    count_r = part_ref.shape[1] // nr
    barrier = pltpu.get_barrier_semaphore()
    for k in range(1, nc):
        pl.semaphore_signal(
            barrier, inc=1, device_id=(r, lax.rem(c + k, nc)), device_id_type=MESH
        )
    for k in range(1, nr):
        pl.semaphore_signal(
            barrier, inc=1, device_id=(lax.rem(r + k, nr), c), device_id_type=MESH
        )
    pl.semaphore_wait(barrier, nc + nr - 2)

    def spread(src, dst, send, recv, count, along_col):
        copies = []
        for k in range(1, count):
            peer = lax.rem((c if along_col else r) + k, count)
            copy = pltpu.make_async_remote_copy(
                src_ref=src(peer),
                dst_ref=dst(k),
                send_sem=send.at[k - 1],
                recv_sem=recv.at[k - 1],
                device_id=(r, peer) if along_col else (peer, c),
                device_id_type=MESH,
            )
            copy.start()
            copies.append(copy)
        return copies

    low, high = channels, channels + NH
    first = spread(lambda p: part_ref.at[p], lambda k: col_buf.at[k - 1], send_1, recv_1, nc, True)
    for copy in first:
        copy.wait()
    owner = owners(part_ref.shape[1:], channels)
    pieces = [part_ref[c]] + [col_buf[k] for k in range(nc - 1)]
    total = join(pieces, owner, low, high)
    for j in range(nr):
        mid[j] = total[j * count_r : (j + 1) * count_r]
    second = spread(lambda p: mid.at[p], lambda k: row_buf.at[k - 1], send_2, recv_2, nr, False)
    for copy in second:
        copy.wait()
    owner = owners(mid.shape[1:], channels)
    pieces = [mid[r]] + [row_buf[k] for k in range(nr - 1)]
    total = join(pieces, owner, low, high)
    divisor = jnp.ones_like(total)
    for head in range(NH):
        divisor = jnp.where(owner == head, total[:, low + head : low + head + 1], divisor)
    pooled = total / divisor
    gathered[c, r] = pooled[:, 0:channels].astype(jnp.bfloat16)
    third = spread(
        lambda p: gathered.at[c, r], lambda k: gathered.at[c, r], send_3, recv_3, nr, False
    )
    for copy in third:
        copy.wait()
    fourth = spread(lambda p: gathered.at[c], lambda k: gathered.at[c], send_4, recv_4, nc, True)
    for copy in fourth:
        copy.wait()
    out_ref[...] = gathered[...]


def merged(part, channels):
    nr, nc = lax.axis_size("row"), lax.axis_size("col")
    count_c = part.shape[0] // nc
    count_r = count_c // nr
    wide = part.shape[1]
    whole = pl.BlockSpec(memory_space=pltpu.VMEM)
    sems = []
    for n in (nc, nr, nr, nc):
        sems += [pltpu.SemaphoreType.DMA((n - 1,))] * 2
    pooled = pl.pallas_call(
        functools.partial(merge_kernel, nr, nc, channels),
        out_shape=jax.ShapeDtypeStruct((nc, nr, count_r, channels), jnp.bfloat16),
        in_specs=[whole],
        out_specs=whole,
        scratch_shapes=[
            pltpu.VMEM((nc - 1, count_c, wide), jnp.float32),
            pltpu.VMEM((nr, count_r, wide), jnp.float32),
            pltpu.VMEM((nr - 1, count_r, wide), jnp.float32),
            pltpu.VMEM((nc, nr, count_r, channels), jnp.bfloat16),
        ]
        + sems,
        compiler_params=pltpu.CompilerParams(collective_id=0, has_side_effects=True),
        name="merge",
    )(part.reshape(nc, count_c, wide))
    return pooled.reshape(part.shape[0], channels)


SIDES = [(-1, 0), (1, 0), (0, -1), (0, 1), (-1, -1), (-1, 1), (1, -1), (1, 1)]


def halo_kernel(
    nr,
    nc,
    x_ref,
    above_out,
    below_out,
    left_out,
    right_out,
    above,
    below,
    left,
    right,
    send,
    recv,
):
    r, c = lax.axis_index("row"), lax.axis_index("col")
    rows, cols = x_ref.shape[0], x_ref.shape[1]

    def inside(dr, dc):
        return (r + dr >= 0) & (r + dr < nr) & (c + dc >= 0) & (c + dc < nc)

    barrier = pltpu.get_barrier_semaphore()
    count = 0
    for dr, dc in SIDES:
        valid = inside(dr, dc)
        count = count + jnp.where(valid, 1, 0)

        @pl.when(valid)
        def _(dr=dr, dc=dc):
            pl.semaphore_signal(barrier, inc=1, device_id=(r + dr, c + dc), device_id_type=MESH)

    pl.semaphore_wait(barrier, count)

    def source(dr, dc):
        at = {-1: pl.ds(0, 3), 0: pl.ds(0, rows), 1: pl.ds(rows - 3, 3)}[dr]
        to = {-1: pl.ds(0, PAD), 0: pl.ds(0, cols), 1: pl.ds(cols - PAD, PAD)}[dc]
        return x_ref.at[at, to]

    def target(dr, dc):
        if dc == 0:
            return below if dr < 0 else above
        strip = right if dc < 0 else left
        at = {-1: pl.ds(rows + 3, 3), 0: pl.ds(3, rows), 1: pl.ds(0, 3)}[dr]
        return strip.at[at]

    def copy(d):
        dr, dc = SIDES[d]
        return pltpu.make_async_remote_copy(
            src_ref=source(dr, dc),
            dst_ref=target(dr, dc),
            send_sem=send.at[d],
            recv_sem=recv.at[d],
            device_id=(r + dr, c + dc),
            device_id_type=MESH,
        )

    for d, (dr, dc) in enumerate(SIDES):

        @pl.when(inside(dr, dc))
        def _(d=d):
            copy(d).start()

    for d, (dr, dc) in enumerate(SIDES):

        @pl.when(jnp.logical_not(inside(-dr, -dc)))
        def _(dr=dr, dc=dc):
            place = target(dr, dc)
            place[...] = jnp.zeros(place.shape, place.dtype)

    for d, (dr, dc) in enumerate(SIDES):

        @pl.when(inside(-dr, -dc))
        def _(d=d):
            copy(d).wait_recv()

    above_out[...] = above[...]
    below_out[...] = below[...]
    left_out[...] = left[...]
    right_out[...] = right[...]
    for d, (dr, dc) in enumerate(SIDES):

        @pl.when(inside(dr, dc))
        def _(d=d):
            copy(d).wait_send()


def halo(feature):
    nr, nc = lax.axis_size("row"), lax.axis_size("col")
    rows, cols, channels = feature.shape
    whole = pl.BlockSpec(memory_space=pltpu.VMEM)
    shapes = [(3, cols, channels)] * 2 + [(rows + 6, PAD, channels)] * 2
    return pl.pallas_call(
        functools.partial(halo_kernel, nr, nc),
        out_shape=[jax.ShapeDtypeStruct(shape, feature.dtype) for shape in shapes],
        in_specs=[whole],
        out_specs=[whole] * 4,
        scratch_shapes=[pltpu.VMEM(shape, feature.dtype) for shape in shapes]
        + [pltpu.SemaphoreType.DMA((8,)), pltpu.SemaphoreType.DMA((8,))],
        compiler_params=pltpu.CompilerParams(collective_id=1, has_side_effects=True),
        name="halo",
    )(feature)


def body(
    feature,
    mask,
    dw_weight,
    dw_bias,
    ln_gain,
    ln_bias,
    w_in,
    b_in,
    w_out,
    b_out,
    layer_scale,
    w_key,
    w_value,
    queries,
    w_proj,
):
    rows, cols, channels = feature.shape
    positions = rows * cols
    hidden = w_in.shape[1]
    query_count = queries.shape[0]
    depth = channels + 16
    above, below, left, right = halo(feature)
    bias = jnp.where(mask > 0, 0.0, MASKED).astype(jnp.bfloat16).reshape(1, positions)
    bias = jnp.pad(bias, ((0, 15), (0, 0)))
    qb = 256
    whole = pl.BlockSpec(memory_space=pltpu.VMEM)
    block_out, part = pl.pallas_call(
        functools.partial(block_kernel, rows, cols, channels, hidden, query_count),
        out_shape=(
            jax.ShapeDtypeStruct((rows, channels, cols), jnp.bfloat16),
            jax.ShapeDtypeStruct((query_count, 256), jnp.float32),
        ),
        in_specs=[whole] * 18,
        out_specs=(whole, whole),
        scratch_shapes=[
            pltpu.VMEM((2, 7, 7, 8, 128), jnp.float32),
            pltpu.VMEM((NH * query_count, depth), jnp.bfloat16),
            pltpu.VMEM((channels, channels), jnp.bfloat16),
            pltpu.VMEM((2, rows + 6, cols + 2 * PAD, 128), jnp.float32),
            pltpu.VMEM((rows, cols, 256), jnp.float32),
            pltpu.VMEM((depth, positions), jnp.bfloat16),
            pltpu.VMEM((positions, 256), jnp.bfloat16),
            pltpu.VMEM((qb, positions), jnp.float32),
            pltpu.VMEM((qb, positions), jnp.float32),
        ],
        compiler_params=pltpu.CompilerParams(vmem_limit_bytes=56 << 20),
        name="block",
    )(
        feature,
        above,
        below,
        left,
        right,
        bias,
        dw_weight,
        dw_bias,
        ln_gain,
        ln_bias,
        b_out,
        layer_scale,
        w_in,
        b_in,
        w_out,
        w_key,
        w_value,
        queries,
    )
    pooled_out = jnp.dot(
        merged(part, channels), w_proj, preferred_element_type=jnp.float32
    )
    return (jnp.transpose(block_out, (0, 2, 1)), pooled_out)


def solution(mesh):
    return jax.shard_map(
        body,
        mesh=mesh,
        in_specs=(P("row", "col", None), P("row", "col")) + (P(),) * 13,
        out_specs=(P("row", "col", None), P()),
        check_vma=False,
    )
```

```python
import functools
import math

import jax
import jax.numpy as jnp
from jax import lax
from jax.experimental import pallas as pl
from jax.experimental.pallas import tpu as pltpu
from jax.sharding import PartitionSpec as P

NH = 8
PAD = 16
LOW = -1e29
MASKED = -1e30


def block_kernel(
    rows,
    cols,
    channels,
    hidden,
    query_count,
    x_ref,
    above_ref,
    below_ref,
    above_high_ref,
    below_high_ref,
    left_ref,
    right_ref,
    bias_ref,
    dw_raw_ref,
    dw_bias_ref,
    gain_ref,
    shift_ref,
    b_out_ref,
    scale_ref,
    win_ref,
    bin_ref,
    wout_ref,
    wk_ref,
    wv_ref,
    q_raw_ref,
    out_ref,
    part_ref,
    dw_ref,
    q_ref,
    wkt_ref,
    xf_ref,
    conv_ref,
    kt_ref,
    v_ref,
    sa_ref,
    sb_ref,
):
    positions = rows * cols
    head_size = channels // NH
    depth = kt_ref.shape[0]
    wide = 256
    high = channels - 128

    def place(i, start, size, line):
        line = line.astype(jnp.float32)
        xf_ref[0, i, start : start + size] = line[:, 0:128]
        xf_ref[1, i, start : start + size, 0:high] = line[:, 128:channels]

    def widen(i, carry):
        place(i + 3, PAD, cols, x_ref[i])
        return carry

    def sides(i, carry):
        place(i, 0, PAD, left_ref[i])
        place(i, PAD + cols, PAD, right_ref[i])
        return carry

    lax.fori_loop(0, rows, widen, 0)
    lax.fori_loop(0, rows + 6, sides, 0)
    half_cols = cols // 2
    for i in range(3):
        for base, low_ref, high_ref in (
            (0, above_ref, above_high_ref),
            (rows + 3, below_ref, below_high_ref),
        ):
            xf_ref[0, base + i, PAD : PAD + cols] = low_ref[i].astype(jnp.float32)
            line = high_ref[i].astype(jnp.float32)
            xf_ref[1, base + i, PAD : PAD + half_cols, 0:high] = line[:, 0:high]
            xf_ref[1, base + i, PAD + half_cols : PAD + cols, 0:high] = line[:, high : 2 * high]
    for i in range(7):
        for j in range(7):
            dw_ref[0, i, j] = jnp.broadcast_to(dw_raw_ref[i, j : j + 1, 0:128], (8, 128))
            dw_ref[1, i, j, :, 0:high] = jnp.broadcast_to(
                dw_raw_ref[i, j : j + 1, 128:channels], (8, high)
            )
    wkt_ref[...] = jnp.transpose(wk_ref[...].astype(jnp.float32)).astype(jnp.bfloat16)
    q_lane = lax.broadcasted_iota(jnp.int32, (query_count, channels), 1) // head_size
    tail_lane = lax.broadcasted_iota(jnp.int32, (query_count, depth - channels), 1)
    q_tail = jnp.where(tail_lane == 0, 1.0, 0.0).astype(jnp.bfloat16)
    q_all = q_raw_ref[...].astype(jnp.float32)
    for head in range(NH):
        at = head * query_count
        own = jnp.where(q_lane == head, q_all, 0.0).astype(jnp.bfloat16)
        q_ref[at : at + query_count, 0:channels] = own
        q_ref[at : at + query_count, channels:depth] = q_tail

    def conv_tile(tile, carry):
        start = pl.multiple_of(tile * 8, 8)
        for half in range(2):
            acc = [None] * rows
            for b in range(7):
                taps = [dw_ref[half, a, b] for a in range(7)]
                for i in range(rows + 6):
                    window = xf_ref[half, i, pl.ds(start + (PAD - 3 + b), 8), :]
                    for a in range(7):
                        r = i - a
                        if 0 <= r < rows:
                            term = window * taps[a]
                            acc[r] = term if acc[r] is None else acc[r] + term
            for r in range(rows):
                conv_ref[r, pl.ds(start, 8), half * 128 : half * 128 + 128] = acc[r]
        return carry

    lax.fori_loop(0, cols // 8, conv_tile, 0)

    block = 2 * cols
    dw_bias = dw_bias_ref[...][None, :]
    gain = gain_ref[...][None, :]
    shift = shift_ref[...][None, :]
    b_out = b_out_ref[...][None, :]
    scale = scale_ref[...][None, :]
    b_in = bin_ref[...][None, :]
    kt_ref[channels:depth, :] = jnp.zeros((depth - channels, positions), jnp.bfloat16)
    kt_ref[channels : channels + 16, :] = bias_ref[...]
    lane16 = lax.broadcasted_iota(jnp.int32, (positions, wide - channels), 1)
    v_ref[:, channels:wide] = jnp.where(lane16 < NH, 1.0, 0.0).astype(jnp.bfloat16)

    def mlp(step, carry):
        row = step * 2
        flat = conv_ref[pl.ds(row, 2)].reshape(block, wide)[:, 0:channels] + dw_bias
        center = x_ref[pl.ds(row, 2)].reshape(block, channels)
        average = jnp.mean(flat, axis=-1, keepdims=True)
        moved = flat - average
        spread = jnp.mean(moved * moved, axis=-1, keepdims=True)
        normed = (moved * lax.rsqrt(spread + 1e-06) * gain + shift).astype(jnp.bfloat16)
        inner = jnp.dot(normed, win_ref[...], preferred_element_type=jnp.float32) + b_in
        act = (0.5 * inner * (1.0 + lax.erf(inner * math.sqrt(0.5)))).astype(jnp.bfloat16)
        branch = jnp.dot(act, wout_ref[...], preferred_element_type=jnp.float32) + b_out
        summed = center.astype(jnp.float32) + scale * branch
        result = summed.astype(jnp.bfloat16)
        for i in range(2):
            line = jnp.transpose(summed[i * cols : (i + 1) * cols])
            out_ref[row + i] = line.astype(jnp.bfloat16)
        first = pl.multiple_of(step * block, block)
        kt_ref[0:channels, pl.ds(first, block)] = lax.dot_general(
            wkt_ref[...], result, (((1,), (1,)), ((), ())), preferred_element_type=jnp.float32
        ).astype(jnp.bfloat16)
        v_ref[pl.ds(first, block), 0:channels] = jnp.dot(
            result, wv_ref[...], preferred_element_type=jnp.float32
        ).astype(jnp.bfloat16)
        return carry

    lax.fori_loop(0, rows // 2, mlp, 0)

    factor = math.log2(math.e) / math.sqrt(head_size)
    qb = sa_ref.shape[0]
    blocks = query_count // qb
    total = NH * blocks
    lane = lax.broadcasted_iota(jnp.int32, (qb, wide), 1)
    owner = jnp.where(
        lane < channels,
        lane // head_size,
        jnp.where(lane < channels + NH, lane - channels, NH),
    )

    def score(index, s_ref):
        first = pl.multiple_of(index * qb, qb)
        s = jnp.dot(
            q_ref[pl.ds(first, qb), :], kt_ref[...], preferred_element_type=jnp.float32
        )
        s_ref[...] = s
        return jnp.maximum(jnp.max(s, axis=-1, keepdims=True), LOW)

    def absorb(index, s_ref, top):
        e = jnp.exp2((s_ref[...] - top) * factor).astype(jnp.bfloat16)
        o = jnp.dot(e, v_ref[...], preferred_element_type=jnp.float32)
        head = index // blocks
        at = pl.multiple_of((index - head * blocks) * qb, qb)
        held = part_ref[pl.ds(at, qb), :]
        held = jnp.where(owner == head, o, held)
        held = jnp.where(lane == channels + NH + head, top * factor, held)
        part_ref[pl.ds(at, qb), :] = held

    part_ref[...] = jnp.zeros_like(part_ref)
    top_a = score(0, sa_ref)

    def attend(pair, top_a):
        index = pair * 2
        top_b = score(index + 1, sb_ref)
        absorb(index, sa_ref, top_a)
        top_a = score(jnp.minimum(index + 2, total - 1), sa_ref)
        absorb(index + 1, sb_ref, top_b)
        return top_a

    lax.fori_loop(0, total // 2, attend, top_a)


MESH = pl.DeviceIdType.MESH


def join(packed, owner, low, high):
    top = packed[0]
    for other in packed[1:]:
        top = jnp.maximum(top, other)
    total = None
    for piece in packed:
        keep = jnp.exp2(piece - top)
        factor = jnp.ones_like(piece)
        for head in range(NH):
            factor = jnp.where(owner == head, keep[:, high + head : high + head + 1], factor)
        term = piece * factor
        total = term if total is None else total + term
    lane = lax.broadcasted_iota(jnp.int32, total.shape, 1)
    return jnp.where(lane >= high, top, total)


def owners(shape, channels):
    lane = lax.broadcasted_iota(jnp.int32, shape, 1)
    return jnp.where(
        lane < channels,
        lane // (channels // NH),
        jnp.where(lane < channels + NH, lane - channels, NH),
    )


def merge_kernel(
    nr,
    nc,
    channels,
    part_ref,
    out_ref,
    col_buf,
    mid,
    row_buf,
    gathered,
    send_1,
    recv_1,
    send_2,
    recv_2,
    send_3,
    recv_3,
    send_4,
    recv_4,
):
    r, c = lax.axis_index("row"), lax.axis_index("col")
    count_r = part_ref.shape[1] // nr
    barrier = pltpu.get_barrier_semaphore()
    for k in range(1, nc):
        pl.semaphore_signal(
            barrier, inc=1, device_id=(r, lax.rem(c + k, nc)), device_id_type=MESH
        )
    for k in range(1, nr):
        pl.semaphore_signal(
            barrier, inc=1, device_id=(lax.rem(r + k, nr), c), device_id_type=MESH
        )
    pl.semaphore_wait(barrier, nc + nr - 2)

    def spread(src, dst, send, recv, count, along_col):
        copies = []
        for k in range(1, count):
            peer = lax.rem((c if along_col else r) + k, count)
            copy = pltpu.make_async_remote_copy(
                src_ref=src(peer),
                dst_ref=dst(k),
                send_sem=send.at[k - 1],
                recv_sem=recv.at[k - 1],
                device_id=(r, peer) if along_col else (peer, c),
                device_id_type=MESH,
            )
            copy.start()
            copies.append(copy)
        return copies

    low, high = channels, channels + NH
    first = spread(lambda p: part_ref.at[p], lambda k: col_buf.at[k - 1], send_1, recv_1, nc, True)
    for copy in first:
        copy.wait()
    owner = owners(part_ref.shape[1:], channels)
    pieces = [part_ref[c]] + [col_buf[k] for k in range(nc - 1)]
    total = join(pieces, owner, low, high)
    for j in range(nr):
        mid[j] = total[j * count_r : (j + 1) * count_r]
    second = spread(lambda p: mid.at[p], lambda k: row_buf.at[k - 1], send_2, recv_2, nr, False)
    for copy in second:
        copy.wait()
    owner = owners(mid.shape[1:], channels)
    pieces = [mid[r]] + [row_buf[k] for k in range(nr - 1)]
    total = join(pieces, owner, low, high)
    divisor = jnp.ones_like(total)
    for head in range(NH):
        divisor = jnp.where(owner == head, total[:, low + head : low + head + 1], divisor)
    pooled = total / divisor
    gathered[c, r] = pooled[:, 0:channels].astype(jnp.bfloat16)
    third = spread(
        lambda p: gathered.at[c, r], lambda k: gathered.at[c, r], send_3, recv_3, nr, False
    )
    for copy in third:
        copy.wait()
    fourth = spread(lambda p: gathered.at[c], lambda k: gathered.at[c], send_4, recv_4, nc, True)
    for copy in fourth:
        copy.wait()
    out_ref[...] = gathered[...]


def merged(part, channels):
    nr, nc = lax.axis_size("row"), lax.axis_size("col")
    count_c = part.shape[0] // nc
    count_r = count_c // nr
    wide = part.shape[1]
    whole = pl.BlockSpec(memory_space=pltpu.VMEM)
    sems = []
    for n in (nc, nr, nr, nc):
        sems += [pltpu.SemaphoreType.DMA((n - 1,))] * 2
    pooled = pl.pallas_call(
        functools.partial(merge_kernel, nr, nc, channels),
        out_shape=jax.ShapeDtypeStruct((nc, nr, count_r, channels), jnp.bfloat16),
        in_specs=[whole],
        out_specs=whole,
        scratch_shapes=[
            pltpu.VMEM((nc - 1, count_c, wide), jnp.float32),
            pltpu.VMEM((nr, count_r, wide), jnp.float32),
            pltpu.VMEM((nr - 1, count_r, wide), jnp.float32),
            pltpu.VMEM((nc, nr, count_r, channels), jnp.bfloat16),
        ]
        + sems,
        compiler_params=pltpu.CompilerParams(collective_id=0, has_side_effects=True),
        name="merge",
    )(part.reshape(nc, count_c, wide))
    return pooled.reshape(part.shape[0], channels)


SIDES = [(-1, 0), (1, 0), (0, -1), (0, 1), (-1, -1), (-1, 1), (1, -1), (1, 1)]


def halo_kernel(
    nr,
    nc,
    x_ref,
    above_out,
    below_out,
    above_high_out,
    below_high_out,
    left_out,
    right_out,
    above,
    below,
    above_high,
    below_high,
    left,
    right,
    packed,
    send,
    recv,
    send_high,
    recv_high,
):
    r, c = lax.axis_index("row"), lax.axis_index("col")
    rows, cols, channels = x_ref.shape
    high, half_cols = channels - 128, cols // 2

    def inside(dr, dc):
        return (r + dr >= 0) & (r + dr < nr) & (c + dc >= 0) & (c + dc < nc)

    barrier = pltpu.get_barrier_semaphore()
    count = 0
    for dr, dc in SIDES:
        valid = inside(dr, dc)
        count = count + jnp.where(valid, 1, 0)

        @pl.when(valid)
        def _(dr=dr, dc=dc):
            pl.semaphore_signal(barrier, inc=1, device_id=(r + dr, c + dc), device_id_type=MESH)

    for i in range(3):
        for edge, row in ((0, i), (1, rows - 3 + i)):
            line = x_ref[row, :, 128:channels]
            packed[edge, i, :, 0:high] = line[0:half_cols]
            packed[edge, i, :, high : 2 * high] = line[half_cols:cols]
    pl.semaphore_wait(barrier, count)

    def source(dr, dc):
        at = {-1: pl.ds(0, 3), 0: pl.ds(0, rows), 1: pl.ds(rows - 3, 3)}[dr]
        to = {-1: pl.ds(0, PAD), 0: pl.ds(0, cols), 1: pl.ds(cols - PAD, PAD)}[dc]
        if dc == 0:
            return x_ref.at[at, to, pl.ds(0, 128)]
        return x_ref.at[at, to]

    def target(dr, dc):
        if dc == 0:
            return below if dr < 0 else above
        strip = right if dc < 0 else left
        at = {-1: pl.ds(rows + 3, 3), 0: pl.ds(3, rows), 1: pl.ds(0, 3)}[dr]
        return strip.at[at]

    def copy(d):
        dr, dc = SIDES[d]
        return pltpu.make_async_remote_copy(
            src_ref=source(dr, dc),
            dst_ref=target(dr, dc),
            send_sem=send.at[d],
            recv_sem=recv.at[d],
            device_id=(r + dr, c + dc),
            device_id_type=MESH,
        )

    def copy_high(d):
        dr, dc = SIDES[d]
        return pltpu.make_async_remote_copy(
            src_ref=packed.at[0 if dr < 0 else 1],
            dst_ref=below_high if dr < 0 else above_high,
            send_sem=send_high.at[d],
            recv_sem=recv_high.at[d],
            device_id=(r + dr, c + dc),
            device_id_type=MESH,
        )

    for d, (dr, dc) in enumerate(SIDES):

        @pl.when(inside(dr, dc))
        def _(d=d, dc=dc):
            copy(d).start()
            if dc == 0:
                copy_high(d).start()

    for d, (dr, dc) in enumerate(SIDES):

        @pl.when(jnp.logical_not(inside(-dr, -dc)))
        def _(dr=dr, dc=dc):
            place = target(dr, dc)
            place[...] = jnp.zeros(place.shape, place.dtype)
            if dc == 0:
                other = below_high if dr < 0 else above_high
                other[...] = jnp.zeros(other.shape, other.dtype)

    for d, (dr, dc) in enumerate(SIDES):

        @pl.when(inside(-dr, -dc))
        def _(d=d, dc=dc):
            copy(d).wait_recv()
            if dc == 0:
                copy_high(d).wait_recv()

    above_out[...] = above[...]
    below_out[...] = below[...]
    above_high_out[...] = above_high[...]
    below_high_out[...] = below_high[...]
    left_out[...] = left[...]
    right_out[...] = right[...]
    for d, (dr, dc) in enumerate(SIDES):

        @pl.when(inside(dr, dc))
        def _(d=d, dc=dc):
            copy(d).wait_send()
            if dc == 0:
                copy_high(d).wait_send()


def halo(feature):
    nr, nc = lax.axis_size("row"), lax.axis_size("col")
    rows, cols, channels = feature.shape
    whole = pl.BlockSpec(memory_space=pltpu.VMEM)
    high_shape = (3, cols // 2, 2 * (channels - 128))
    shapes = [(3, cols, 128)] * 2 + [high_shape] * 2 + [(rows + 6, PAD, channels)] * 2
    return pl.pallas_call(
        functools.partial(halo_kernel, nr, nc),
        out_shape=[jax.ShapeDtypeStruct(shape, feature.dtype) for shape in shapes],
        in_specs=[whole],
        out_specs=[whole] * 6,
        scratch_shapes=[pltpu.VMEM(shape, feature.dtype) for shape in shapes]
        + [pltpu.VMEM((2,) + high_shape, feature.dtype)]
        + [pltpu.SemaphoreType.DMA((8,))] * 2
        + [pltpu.SemaphoreType.DMA((2,))] * 2,
        compiler_params=pltpu.CompilerParams(collective_id=1, has_side_effects=True),
        name="halo",
    )(feature)


def body(
    feature,
    mask,
    dw_weight,
    dw_bias,
    ln_gain,
    ln_bias,
    w_in,
    b_in,
    w_out,
    b_out,
    layer_scale,
    w_key,
    w_value,
    queries,
    w_proj,
):
    rows, cols, channels = feature.shape
    positions = rows * cols
    hidden = w_in.shape[1]
    query_count = queries.shape[0]
    depth = channels + 16
    strips = halo(feature)
    bias = jnp.where(mask > 0, 0.0, MASKED).astype(jnp.bfloat16).reshape(1, positions)
    bias = jnp.pad(bias, ((0, 15), (0, 0)))
    qb = 256
    whole = pl.BlockSpec(memory_space=pltpu.VMEM)
    block_out, part = pl.pallas_call(
        functools.partial(block_kernel, rows, cols, channels, hidden, query_count),
        out_shape=(
            jax.ShapeDtypeStruct((rows, channels, cols), jnp.bfloat16),
            jax.ShapeDtypeStruct((query_count, 256), jnp.float32),
        ),
        in_specs=[whole] * 20,
        out_specs=(whole, whole),
        scratch_shapes=[
            pltpu.VMEM((2, 7, 7, 8, 128), jnp.float32),
            pltpu.VMEM((NH * query_count, depth), jnp.bfloat16),
            pltpu.VMEM((channels, channels), jnp.bfloat16),
            pltpu.VMEM((2, rows + 6, cols + 2 * PAD, 128), jnp.float32),
            pltpu.VMEM((rows, cols, 256), jnp.float32),
            pltpu.VMEM((depth, positions), jnp.bfloat16),
            pltpu.VMEM((positions, 256), jnp.bfloat16),
            pltpu.VMEM((qb, positions), jnp.float32),
            pltpu.VMEM((qb, positions), jnp.float32),
        ],
        compiler_params=pltpu.CompilerParams(vmem_limit_bytes=56 << 20),
        name="block",
    )(
        feature,
        *strips,
        bias,
        dw_weight,
        dw_bias,
        ln_gain,
        ln_bias,
        b_out,
        layer_scale,
        w_in,
        b_in,
        w_out,
        w_key,
        w_value,
        queries,
    )
    pooled_out = jnp.dot(
        merged(part, channels), w_proj, preferred_element_type=jnp.float32
    )
    return (jnp.transpose(block_out, (0, 2, 1)), pooled_out)


def solution(mesh):
    return jax.shard_map(
        body,
        mesh=mesh,
        in_specs=(P("row", "col", None), P("row", "col")) + (P(),) * 13,
        out_specs=(P("row", "col", None), P()),
        check_vma=False,
    )
```

```python
import functools
import math

import jax
import jax.numpy as jnp
from jax import lax
from jax.experimental import pallas as pl
from jax.experimental.pallas import tpu as pltpu
from jax.sharding import PartitionSpec as P

NH = 8
PAD = 16
LOW = -1e29
MASKED = -1e30


def block_kernel(
    rows,
    cols,
    channels,
    hidden,
    query_count,
    x_ref,
    above_ref,
    below_ref,
    above_high_ref,
    below_high_ref,
    left_ref,
    right_ref,
    bias_ref,
    dw_raw_ref,
    dw_bias_ref,
    gain_ref,
    shift_ref,
    b_out_ref,
    scale_ref,
    win_ref,
    bin_ref,
    wout_ref,
    wk_ref,
    wv_ref,
    q_raw_ref,
    out_ref,
    part_ref,
    dw_ref,
    q_ref,
    wkt_ref,
    xf_ref,
    conv_ref,
    kt_ref,
    v_ref,
    sa_ref,
    sb_ref,
):
    positions = rows * cols
    head_size = channels // NH
    depth = kt_ref.shape[0]
    wide = 256
    high = channels - 128

    def place(i, start, size, line):
        line = line.astype(jnp.float32)
        xf_ref[0, i, start : start + size] = line[:, 0:128]
        xf_ref[1, i, start : start + size, 0:high] = line[:, 128:channels]

    def widen(i, carry):
        place(i + 3, PAD, cols, x_ref[i])
        return carry

    def sides(i, carry):
        place(i, 0, PAD, left_ref[i])
        place(i, PAD + cols, PAD, right_ref[i])
        return carry

    lax.fori_loop(0, rows, widen, 0)
    lax.fori_loop(0, rows + 6, sides, 0)
    half_cols = cols // 2
    for i in range(3):
        for base, low_ref, high_ref in (
            (0, above_ref, above_high_ref),
            (rows + 3, below_ref, below_high_ref),
        ):
            xf_ref[0, base + i, PAD : PAD + cols] = low_ref[i].astype(jnp.float32)
            line = high_ref[i].astype(jnp.float32)
            xf_ref[1, base + i, PAD : PAD + half_cols, 0:high] = line[:, 0:high]
            xf_ref[1, base + i, PAD + half_cols : PAD + cols, 0:high] = line[:, high : 2 * high]
    for i in range(7):
        for j in range(7):
            dw_ref[0, i, j] = jnp.broadcast_to(dw_raw_ref[i, j : j + 1, 0:128], (8, 128))
            dw_ref[1, i, j, :, 0:high] = jnp.broadcast_to(
                dw_raw_ref[i, j : j + 1, 128:channels], (8, high)
            )
    wkt_ref[...] = jnp.transpose(wk_ref[...].astype(jnp.float32)).astype(jnp.bfloat16)
    q_lane = lax.broadcasted_iota(jnp.int32, (query_count, channels), 1) // head_size
    tail_lane = lax.broadcasted_iota(jnp.int32, (query_count, depth - channels), 1)
    q_tail = jnp.where(tail_lane == 0, 1.0, 0.0).astype(jnp.bfloat16)
    q_all = jnp.transpose(q_raw_ref[...].astype(jnp.float32))
    for head in range(NH):
        at = head * query_count
        own = jnp.where(q_lane == head, q_all, 0.0).astype(jnp.bfloat16)
        q_ref[at : at + query_count, 0:channels] = own
        q_ref[at : at + query_count, channels:depth] = q_tail

    def conv_tile(tile, carry):
        start = pl.multiple_of(tile * 8, 8)
        for half in range(2):
            acc = [None] * rows
            for b in range(7):
                taps = [dw_ref[half, a, b] for a in range(7)]
                for i in range(rows + 6):
                    window = xf_ref[half, i, pl.ds(start + (PAD - 3 + b), 8), :]
                    for a in range(7):
                        r = i - a
                        if 0 <= r < rows:
                            term = window * taps[a]
                            acc[r] = term if acc[r] is None else acc[r] + term
            for r in range(rows):
                conv_ref[r, pl.ds(start, 8), half * 128 : half * 128 + 128] = acc[r]
        return carry

    lax.fori_loop(0, cols // 8, conv_tile, 0)

    block = 2 * cols
    dw_bias = dw_bias_ref[...][None, :]
    gain = gain_ref[...][None, :]
    shift = shift_ref[...][None, :]
    b_out = b_out_ref[...][None, :]
    scale = scale_ref[...][None, :]
    b_in = bin_ref[...][None, :]
    kt_ref[channels:depth, :] = jnp.zeros((depth - channels, positions), jnp.bfloat16)
    kt_ref[channels : channels + 16, :] = bias_ref[...]
    lane16 = lax.broadcasted_iota(jnp.int32, (positions, wide - channels), 1)
    v_ref[:, channels:wide] = jnp.where(lane16 < NH, 1.0, 0.0).astype(jnp.bfloat16)

    def mlp(step, carry):
        row = step * 2
        flat = conv_ref[pl.ds(row, 2)].reshape(block, wide)[:, 0:channels] + dw_bias
        center = x_ref[pl.ds(row, 2)].reshape(block, channels)
        average = jnp.mean(flat, axis=-1, keepdims=True)
        moved = flat - average
        spread = jnp.mean(moved * moved, axis=-1, keepdims=True)
        normed = (moved * lax.rsqrt(spread + 1e-06) * gain + shift).astype(jnp.bfloat16)
        inner = jnp.dot(normed, win_ref[...], preferred_element_type=jnp.float32) + b_in
        act = (0.5 * inner * (1.0 + lax.erf(inner * math.sqrt(0.5)))).astype(jnp.bfloat16)
        branch = lax.dot_general(
            act, wout_ref[...], (((1,), (1,)), ((), ())), preferred_element_type=jnp.float32
        )
        branch = branch + b_out
        summed = center.astype(jnp.float32) + scale * branch
        result = summed.astype(jnp.bfloat16)
        for i in range(2):
            line = jnp.transpose(summed[i * cols : (i + 1) * cols])
            out_ref[row + i] = line.astype(jnp.bfloat16)
        first = pl.multiple_of(step * block, block)
        kt_ref[0:channels, pl.ds(first, block)] = lax.dot_general(
            wkt_ref[...], result, (((1,), (1,)), ((), ())), preferred_element_type=jnp.float32
        ).astype(jnp.bfloat16)
        v_ref[pl.ds(first, block), 0:channels] = jnp.dot(
            result, wv_ref[...], preferred_element_type=jnp.float32
        ).astype(jnp.bfloat16)
        return carry

    lax.fori_loop(0, rows // 2, mlp, 0)

    factor = math.log2(math.e) / math.sqrt(head_size)
    qb = sa_ref.shape[0]
    blocks = query_count // qb
    total = NH * blocks
    lane = lax.broadcasted_iota(jnp.int32, (qb, wide), 1)
    owner = jnp.where(
        lane < channels,
        lane // head_size,
        jnp.where(lane < channels + NH, lane - channels, NH),
    )

    def score(index, s_ref):
        first = pl.multiple_of(index * qb, qb)
        s = jnp.dot(
            q_ref[pl.ds(first, qb), :], kt_ref[...], preferred_element_type=jnp.float32
        )
        s_ref[...] = s
        return jnp.maximum(jnp.max(s, axis=-1, keepdims=True), LOW)

    def absorb(index, s_ref, top):
        e = jnp.exp2((s_ref[...] - top) * factor).astype(jnp.bfloat16)
        o = jnp.dot(e, v_ref[...], preferred_element_type=jnp.float32)
        head = index // blocks
        at = pl.multiple_of((index - head * blocks) * qb, qb)
        held = part_ref[pl.ds(at, qb), :]
        held = jnp.where(owner == head, o, held)
        held = jnp.where(lane == channels + NH + head, top * factor, held)
        part_ref[pl.ds(at, qb), :] = held

    part_ref[...] = jnp.zeros_like(part_ref)
    top_a = score(0, sa_ref)

    def attend(pair, top_a):
        index = pair * 2
        top_b = score(index + 1, sb_ref)
        absorb(index, sa_ref, top_a)
        top_a = score(jnp.minimum(index + 2, total - 1), sa_ref)
        absorb(index + 1, sb_ref, top_b)
        return top_a

    lax.fori_loop(0, total // 2, attend, top_a)


MESH = pl.DeviceIdType.MESH


def join(packed, owner, low, high):
    top = packed[0]
    for other in packed[1:]:
        top = jnp.maximum(top, other)
    total = None
    for piece in packed:
        keep = jnp.exp2(piece - top)
        factor = jnp.ones_like(piece)
        for head in range(NH):
            factor = jnp.where(owner == head, keep[:, high + head : high + head + 1], factor)
        term = piece * factor
        total = term if total is None else total + term
    lane = lax.broadcasted_iota(jnp.int32, total.shape, 1)
    return jnp.where(lane >= high, top, total)


def owners(shape, channels):
    lane = lax.broadcasted_iota(jnp.int32, shape, 1)
    return jnp.where(
        lane < channels,
        lane // (channels // NH),
        jnp.where(lane < channels + NH, lane - channels, NH),
    )


def merge_kernel(
    nr,
    nc,
    channels,
    part_ref,
    out_ref,
    col_buf,
    mid,
    row_buf,
    gathered,
    send_1,
    recv_1,
    send_2,
    recv_2,
    send_3,
    recv_3,
    send_4,
    recv_4,
):
    r, c = lax.axis_index("row"), lax.axis_index("col")
    count_r = part_ref.shape[1] // nr
    barrier = pltpu.get_barrier_semaphore()
    for k in range(1, nc):
        pl.semaphore_signal(
            barrier, inc=1, device_id=(r, lax.rem(c + k, nc)), device_id_type=MESH
        )
    for k in range(1, nr):
        pl.semaphore_signal(
            barrier, inc=1, device_id=(lax.rem(r + k, nr), c), device_id_type=MESH
        )
    pl.semaphore_wait(barrier, nc + nr - 2)

    def spread(src, dst, send, recv, count, along_col):
        copies = []
        for k in range(1, count):
            peer = lax.rem((c if along_col else r) + k, count)
            copy = pltpu.make_async_remote_copy(
                src_ref=src(peer),
                dst_ref=dst(k),
                send_sem=send.at[k - 1],
                recv_sem=recv.at[k - 1],
                device_id=(r, peer) if along_col else (peer, c),
                device_id_type=MESH,
            )
            copy.start()
            copies.append(copy)
        return copies

    low, high = channels, channels + NH
    first = spread(lambda p: part_ref.at[p], lambda k: col_buf.at[k - 1], send_1, recv_1, nc, True)
    for copy in first:
        copy.wait()
    owner = owners(part_ref.shape[1:], channels)
    pieces = [part_ref[c]] + [col_buf[k] for k in range(nc - 1)]
    total = join(pieces, owner, low, high)
    for j in range(nr):
        mid[j] = total[j * count_r : (j + 1) * count_r]
    second = spread(lambda p: mid.at[p], lambda k: row_buf.at[k - 1], send_2, recv_2, nr, False)
    for copy in second:
        copy.wait()
    owner = owners(mid.shape[1:], channels)
    pieces = [mid[r]] + [row_buf[k] for k in range(nr - 1)]
    total = join(pieces, owner, low, high)
    divisor = jnp.ones_like(total)
    for head in range(NH):
        divisor = jnp.where(owner == head, total[:, low + head : low + head + 1], divisor)
    pooled = total / divisor
    gathered[c, r] = pooled[:, 0:channels].astype(jnp.bfloat16)
    third = spread(
        lambda p: gathered.at[c, r], lambda k: gathered.at[c, r], send_3, recv_3, nr, False
    )
    for copy in third:
        copy.wait()
    fourth = spread(lambda p: gathered.at[c], lambda k: gathered.at[c], send_4, recv_4, nc, True)
    for copy in fourth:
        copy.wait()
    out_ref[...] = gathered[...]


def merged(part, channels):
    nr, nc = lax.axis_size("row"), lax.axis_size("col")
    count_c = part.shape[0] // nc
    count_r = count_c // nr
    wide = part.shape[1]
    whole = pl.BlockSpec(memory_space=pltpu.VMEM)
    sems = []
    for n in (nc, nr, nr, nc):
        sems += [pltpu.SemaphoreType.DMA((n - 1,))] * 2
    pooled = pl.pallas_call(
        functools.partial(merge_kernel, nr, nc, channels),
        out_shape=jax.ShapeDtypeStruct((nc, nr, count_r, channels), jnp.bfloat16),
        in_specs=[whole],
        out_specs=whole,
        scratch_shapes=[
            pltpu.VMEM((nc - 1, count_c, wide), jnp.float32),
            pltpu.VMEM((nr, count_r, wide), jnp.float32),
            pltpu.VMEM((nr - 1, count_r, wide), jnp.float32),
            pltpu.VMEM((nc, nr, count_r, channels), jnp.bfloat16),
        ]
        + sems,
        compiler_params=pltpu.CompilerParams(collective_id=0, has_side_effects=True),
        name="merge",
    )(part.reshape(nc, count_c, wide))
    return pooled.reshape(part.shape[0], channels)


SIDES = [(-1, 0), (1, 0), (0, -1), (0, 1), (-1, -1), (-1, 1), (1, -1), (1, 1)]


def halo_kernel(
    nr,
    nc,
    x_ref,
    above_out,
    below_out,
    above_high_out,
    below_high_out,
    left_out,
    right_out,
    above,
    below,
    above_high,
    below_high,
    left,
    right,
    packed,
    send,
    recv,
    send_high,
    recv_high,
):
    r, c = lax.axis_index("row"), lax.axis_index("col")
    rows, cols, channels = x_ref.shape
    high, half_cols = channels - 128, cols // 2

    def inside(dr, dc):
        return (r + dr >= 0) & (r + dr < nr) & (c + dc >= 0) & (c + dc < nc)

    barrier = pltpu.get_barrier_semaphore()
    count = 0
    for dr, dc in SIDES:
        valid = inside(dr, dc)
        count = count + jnp.where(valid, 1, 0)

        @pl.when(valid)
        def _(dr=dr, dc=dc):
            pl.semaphore_signal(barrier, inc=1, device_id=(r + dr, c + dc), device_id_type=MESH)

    for i in range(3):
        for edge, row in ((0, i), (1, rows - 3 + i)):
            line = x_ref[row, :, 128:channels]
            packed[edge, i, :, 0:high] = line[0:half_cols]
            packed[edge, i, :, high : 2 * high] = line[half_cols:cols]
    pl.semaphore_wait(barrier, count)

    def source(dr, dc):
        at = {-1: pl.ds(0, 3), 0: pl.ds(0, rows), 1: pl.ds(rows - 3, 3)}[dr]
        to = {-1: pl.ds(0, PAD), 0: pl.ds(0, cols), 1: pl.ds(cols - PAD, PAD)}[dc]
        if dc == 0:
            return x_ref.at[at, to, pl.ds(0, 128)]
        return x_ref.at[at, to]

    def target(dr, dc):
        if dc == 0:
            return below if dr < 0 else above
        strip = right if dc < 0 else left
        at = {-1: pl.ds(rows + 3, 3), 0: pl.ds(3, rows), 1: pl.ds(0, 3)}[dr]
        return strip.at[at]

    def copy(d):
        dr, dc = SIDES[d]
        return pltpu.make_async_remote_copy(
            src_ref=source(dr, dc),
            dst_ref=target(dr, dc),
            send_sem=send.at[d],
            recv_sem=recv.at[d],
            device_id=(r + dr, c + dc),
            device_id_type=MESH,
        )

    def copy_high(d):
        dr, dc = SIDES[d]
        return pltpu.make_async_remote_copy(
            src_ref=packed.at[0 if dr < 0 else 1],
            dst_ref=below_high if dr < 0 else above_high,
            send_sem=send_high.at[d],
            recv_sem=recv_high.at[d],
            device_id=(r + dr, c + dc),
            device_id_type=MESH,
        )

    for d, (dr, dc) in enumerate(SIDES):

        @pl.when(inside(dr, dc))
        def _(d=d, dc=dc):
            copy(d).start()
            if dc == 0:
                copy_high(d).start()

    for d, (dr, dc) in enumerate(SIDES):

        @pl.when(jnp.logical_not(inside(-dr, -dc)))
        def _(dr=dr, dc=dc):
            place = target(dr, dc)
            place[...] = jnp.zeros(place.shape, place.dtype)
            if dc == 0:
                other = below_high if dr < 0 else above_high
                other[...] = jnp.zeros(other.shape, other.dtype)

    for d, (dr, dc) in enumerate(SIDES):

        @pl.when(inside(-dr, -dc))
        def _(d=d, dc=dc):
            copy(d).wait_recv()
            if dc == 0:
                copy_high(d).wait_recv()

    above_out[...] = above[...]
    below_out[...] = below[...]
    above_high_out[...] = above_high[...]
    below_high_out[...] = below_high[...]
    left_out[...] = left[...]
    right_out[...] = right[...]
    for d, (dr, dc) in enumerate(SIDES):

        @pl.when(inside(dr, dc))
        def _(d=d, dc=dc):
            copy(d).wait_send()
            if dc == 0:
                copy_high(d).wait_send()


def halo(feature):
    nr, nc = lax.axis_size("row"), lax.axis_size("col")
    rows, cols, channels = feature.shape
    whole = pl.BlockSpec(memory_space=pltpu.VMEM)
    high_shape = (3, cols // 2, 2 * (channels - 128))
    shapes = [(3, cols, 128)] * 2 + [high_shape] * 2 + [(rows + 6, PAD, channels)] * 2
    return pl.pallas_call(
        functools.partial(halo_kernel, nr, nc),
        out_shape=[jax.ShapeDtypeStruct(shape, feature.dtype) for shape in shapes],
        in_specs=[whole],
        out_specs=[whole] * 6,
        scratch_shapes=[pltpu.VMEM(shape, feature.dtype) for shape in shapes]
        + [pltpu.VMEM((2,) + high_shape, feature.dtype)]
        + [pltpu.SemaphoreType.DMA((8,))] * 2
        + [pltpu.SemaphoreType.DMA((2,))] * 2,
        compiler_params=pltpu.CompilerParams(collective_id=1, has_side_effects=True),
        name="halo",
    )(feature)


def body(
    feature,
    mask,
    dw_weight,
    dw_bias,
    ln_gain,
    ln_bias,
    w_in,
    b_in,
    w_out,
    b_out,
    layer_scale,
    w_key,
    w_value,
    queries,
    w_proj,
):
    rows, cols, channels = feature.shape
    positions = rows * cols
    hidden = w_in.shape[1]
    query_count = queries.shape[0]
    depth = channels + 16
    strips = halo(feature)
    bias = jnp.where(mask > 0, 0.0, MASKED).astype(jnp.bfloat16).reshape(1, positions)
    bias = jnp.pad(bias, ((0, 15), (0, 0)))
    qb = 256
    whole = pl.BlockSpec(memory_space=pltpu.VMEM)
    block_out, part = pl.pallas_call(
        functools.partial(block_kernel, rows, cols, channels, hidden, query_count),
        out_shape=(
            jax.ShapeDtypeStruct((rows, channels, cols), jnp.bfloat16),
            jax.ShapeDtypeStruct((query_count, 256), jnp.float32),
        ),
        in_specs=[whole] * 20,
        out_specs=(whole, whole),
        scratch_shapes=[
            pltpu.VMEM((2, 7, 7, 8, 128), jnp.float32),
            pltpu.VMEM((NH * query_count, depth), jnp.bfloat16),
            pltpu.VMEM((channels, channels), jnp.bfloat16),
            pltpu.VMEM((2, rows + 6, cols + 2 * PAD, 128), jnp.float32),
            pltpu.VMEM((rows, cols, 256), jnp.float32),
            pltpu.VMEM((depth, positions), jnp.bfloat16),
            pltpu.VMEM((positions, 256), jnp.bfloat16),
            pltpu.VMEM((qb, positions), jnp.float32),
            pltpu.VMEM((qb, positions), jnp.float32),
        ],
        compiler_params=pltpu.CompilerParams(vmem_limit_bytes=56 << 20),
        name="block",
    )(
        feature,
        *strips,
        bias,
        dw_weight,
        dw_bias,
        ln_gain,
        ln_bias,
        b_out,
        layer_scale,
        w_in,
        b_in,
        jnp.transpose(w_out),
        w_key,
        w_value,
        jnp.transpose(queries),
    )
    pooled_out = jnp.dot(
        merged(part, channels), w_proj, preferred_element_type=jnp.float32
    )
    return (jnp.transpose(block_out, (0, 2, 1)), pooled_out)


def solution(mesh):
    return jax.shard_map(
        body,
        mesh=mesh,
        in_specs=(P("row", "col", None), P("row", "col")) + (P(),) * 13,
        out_specs=(P("row", "col", None), P()),
        check_vma=False,
    )
```
